32 devices in a mesh: dp: 8 (over z, y), tensor: 4 (over x, core).
Axes of the slice: x: 2, y: 2, z: 4, core: 2. Of those that a mesh axis runs over, the one named last changes fastest.
Arguments:
- tokens: bfloat16 [4096, 1024], P(('dp', 'tensor')), may hold values from -6 to 6
- segment_ids: int32 [4096], P('dp'), may hold values from 0 to 31, never falling along the last dimension, each value on 1 to 256 neighbouring positions
- norm_gain_mixer: bfloat16 [1024], P('dp'), may hold values from 0.5 to 1.5
- query_weight: bfloat16 [1024, 1024], P('dp', 'tensor'), may hold values from -0.1875 to 0.1875
- key_weight: bfloat16 [1024, 1024], P('dp', 'tensor'), may hold values from -0.1875 to 0.1875
- value_weight: bfloat16 [1024, 2048], P('dp', 'tensor'), may hold values from -0.1875 to 0.1875
- gate_weight: bfloat16 [1024, 2048], P('dp', 'tensor'), may hold values from -0.1875 to 0.1875
- alpha_weight: bfloat16 [1024, 8], P('dp', 'tensor'), may hold values from -0.1875 to 0.1875
- beta_weight: bfloat16 [1024, 8], P('dp', 'tensor'), may hold values from -0.1875 to 0.1875
- conv_query: bfloat16 [4, 8, 128], P(None, 'tensor', 'dp'), may hold values from -3 to 3
- conv_key: bfloat16 [4, 8, 128], P(None, 'tensor', 'dp'), may hold values from -3 to 3
- conv_value: bfloat16 [4, 8, 256], P(None, 'tensor', 'dp'), may hold values from -3 to 3
- decay_log: float32 [8], P('tensor'), may hold values from 0 to 2.7725887
- decay_bias: float32 [8], P('tensor'), may hold values from -6.9073 to -2.2521, as said below
- output_gain: bfloat16 [8, 256], P('tensor', 'dp'), may hold values from 0.5 to 1.5
- output_weight: bfloat16 [2048, 1024], P('tensor', 'dp'), may hold values from -0.125 to 0.125
- norm_gain_ffn: bfloat16 [1024], P('dp'), may hold values from 0.5 to 1.5
- ffn_gate: bfloat16 [1024, 2816], P('dp', 'tensor'), may hold values from -0.1875 to 0.1875
- ffn_up: bfloat16 [1024, 2816], P('dp', 'tensor'), may hold values from -0.1875 to 0.1875
- ffn_down: bfloat16 [2816, 1024], P('tensor', 'dp'), may hold values from -0.109375 to 0.109375
- grad_block: bfloat16 [4096, 1024], P(('dp', 'tensor')), may hold values from -6 to 6
Outputs:
- block_output: bfloat16 [4096, 1024], P(('dp', 'tensor'))
- tokens_grad: float32 [4096, 1024], P(('dp', 'tensor'))
- norm_gain_mixer_grad: float32 [1024], P('dp')
- query_weight_grad: float32 [1024, 1024], P('dp', 'tensor')
- key_weight_grad: float32 [1024, 1024], P('dp', 'tensor')
- value_weight_grad: float32 [1024, 2048], P('dp', 'tensor')
- gate_weight_grad: float32 [1024, 2048], P('dp', 'tensor')
- alpha_weight_grad: float32 [1024, 8], P('dp', 'tensor')
- beta_weight_grad: float32 [1024, 8], P('dp', 'tensor')
- conv_query_grad: float32 [4, 8, 128], P(None, 'tensor', 'dp')
- conv_key_grad: float32 [4, 8, 128], P(None, 'tensor', 'dp')
- conv_value_grad: float32 [4, 8, 256], P(None, 'tensor', 'dp')
- decay_log_grad: float32 [8], P('tensor')
- decay_bias_grad: float32 [8], P('tensor')
- output_gain_grad: float32 [8, 256], P('tensor', 'dp')
- output_weight_grad: float32 [2048, 1024], P('tensor', 'dp')
- norm_gain_ffn_grad: float32 [1024], P('dp')
- ffn_gate_grad: float32 [1024, 2816], P('dp', 'tensor')
- ffn_up_grad: float32 [1024, 2816], P('dp', 'tensor')
- ffn_down_grad: float32 [2816, 1024], P('tensor', 'dp')
The draws below stay inside these ranges and needn't reach their ends.
Inputs may be any that keep to these rules, and one draw needn't show every extreme that they name: `segment_ids`: segment ids never fall along the tokens; a document has at most 256 tokens, and one has exactly that many. `decay_bias`: each entry is log(exp(dt) - 1) for a step size dt between 0.001 and 0.1.
All inputs are finite; a program needn't handle non-finite values.
Results may differ from the reference program's by a relative error of at most 0.013.
Values may be sent and summed in bfloat16 or wider, within the bound.
No kernel may reach another device: no remote copies, remote signals or barrier semaphores. Data moves between devices by JAX's collectives and lax.ppermute only.
A program may use at most 192 MiB of HBM per device.

```python
import math
from functools import partial
import jax
import jax.numpy as jnp
import numpy as np
from jax import lax

D = 1024
H = 8
DK = 128
DV = 256
FF = 2816
KCONV = 4
GROUP = 64
LEN = 512
TOKENS = 4096


def draw_decay_bias(key, part):
    step_log = jax.random.uniform(key, (H,), jnp.float32, math.log(0.001), math.log(0.1))
    step_size = jnp.exp(step_log)
    return jnp.log(jnp.expm1(step_size)).astype(jnp.float32)


def block_levels(own_key, shape, shards, smallest, top_value):
    gain, own = 1.0, jax.random.fold_in(own_key, 6)
    for dim, parts in shards:
        heights = jnp.exp(jax.random.uniform(jax.random.fold_in(own, dim), (parts,), jnp.float32, smallest / len(shards), top_value / len(shards)))
        gain = gain * jnp.repeat(heights, shape[dim] // parts).reshape([-1 if axis == dim else 1 for axis in range(len(shape))])
    return gain


def split_up(count, total, bound, slope):
    portions = [(1 << 20) // math.isqrt(standing ** slope) + 1 for standing in range(2, count + 1)]
    surplus, counts = total - bound - (count - 1), [1] * (count - 1)
    while surplus > 0:
        candidates = [i for i in range(count - 1) if counts[i] < bound]
        whole, left = sum([portions[i] for i in candidates]), surplus
        for i in candidates:
            extra = min(bound - counts[i], max(1, left * portions[i] // whole), surplus)
            counts[i] = counts[i] + extra
            surplus = surplus - extra
    return np.array([bound] + counts)


def uneven(stream_key, number_of, total, most, skew):
    if number_of == 2:
        one = jax.random.randint(stream_key, (), max(1, total - most), min(most, total - 1) + 1)
        return jnp.stack([one, total - one])
    sizes = jnp.asarray(split_up(number_of, total, most, skew), jnp.int32)
    couples = (number_of - 1) // 2
    source_of, receiver = sizes[1:1 + 2 * couples:2], sizes[2:2 + 2 * couples:2]
    room = jnp.minimum(source_of - 1, most - receiver)
    shifted = jax.random.randint(jax.random.fold_in(stream_key, 1), (couples,), 0, 1 << 20) % (room + 1)
    sizes = sizes.at[1:1 + 2 * couples:2].set(source_of - shifted).at[2:2 + 2 * couples:2].set(receiver + shifted)
    return sizes[jax.random.permutation(jax.random.fold_in(stream_key, 2), number_of)]


def normal_values(stream_key, extent, scale, limit, cuts=(), kind=jnp.bfloat16):
    values = jax.random.normal(stream_key, extent, jnp.float32) * scale
    if len(cuts) > 0:
        values = block_levels(stream_key, extent, cuts, -0.22, 0.18) * values
    return jnp.clip(values, min=-limit, max=limit).astype(kind)


def setup_inputs(seed: int = 0) -> dict:
    arg_keys = jax.random.split(jax.random.key(seed), 22)
    tokens = normal_values(arg_keys[0], (TOKENS, D), 1.0, 6.0, ((0, 32),))
    segment_ids = jnp.searchsorted(jnp.cumsum(uneven(arg_keys[1], TOKENS * 4 // LEN, TOKENS, LEN // 2, 1)), jnp.arange(TOKENS), side="right").astype(jnp.int32)
    norm_gain_mixer = jnp.clip(1.0 + 0.1 * jax.random.normal(arg_keys[2], (D,), jnp.float32), 0.5, 1.5).astype(jnp.bfloat16)
    query_weight = normal_values(arg_keys[3], (D, H * DK), D ** -0.5, 0.1875, ((0, 8), (1, 4)))
    key_weight = normal_values(arg_keys[4], (D, H * DK), D ** -0.5, 0.1875, ((0, 8), (1, 4)))
    value_weight = normal_values(arg_keys[5], (D, H * DV), D ** -0.5, 0.1875, ((0, 8), (1, 4)))
    gate_weight = normal_values(arg_keys[6], (D, H * DV), D ** -0.5, 0.1875, ((0, 8), (1, 4)))
    alpha_weight = normal_values(arg_keys[7], (D, H), D ** -0.5, 0.1875, ((0, 8), (1, 4)))
    beta_weight = normal_values(arg_keys[8], (D, H), D ** -0.5, 0.1875, ((0, 8), (1, 4)))
    conv_query = normal_values(arg_keys[9], (KCONV, H, DK), 0.5, 3.0, ((1, 4), (2, 8)))
    conv_key = normal_values(arg_keys[10], (KCONV, H, DK), 0.5, 3.0, ((1, 4), (2, 8)))
    conv_value = normal_values(arg_keys[11], (KCONV, H, DV), 0.5, 3.0, ((1, 4), (2, 8)))
    decay_log = jnp.clip(2.7725887 * jax.random.uniform(arg_keys[12], (H,), jnp.float32) ** block_levels(arg_keys[12], (H,), ((0, 4),), -0.2, 0.2), 0.0, 2.7725887)
    decay_bias = draw_decay_bias(jax.random.fold_in(arg_keys[21], 71), 0)
    output_gain = jnp.clip(1.0 + 0.1 * jax.random.normal(arg_keys[14], (H, DV), jnp.float32), 0.5, 1.5).astype(jnp.bfloat16)
    output_weight = normal_values(arg_keys[15], (H * DV, D), (H * DV) ** -0.5, 0.125, ((0, 4), (1, 8)))
    norm_gain_ffn = jnp.clip(1.0 + 0.1 * jax.random.normal(arg_keys[16], (D,), jnp.float32), 0.5, 1.5).astype(jnp.bfloat16)
    ffn_gate = normal_values(arg_keys[17], (D, FF), D ** -0.5, 0.1875, ((0, 8), (1, 4)))
    ffn_up = normal_values(arg_keys[18], (D, FF), D ** -0.5, 0.1875, ((0, 8), (1, 4)))
    ffn_down = normal_values(arg_keys[19], (FF, D), FF ** -0.5, 0.109375, ((0, 4), (1, 8)))
    grad_block = normal_values(arg_keys[20], (TOKENS, D), 1.0, 6.0, ((0, 32),))
    return dict(tokens=tokens, segment_ids=segment_ids, norm_gain_mixer=norm_gain_mixer, query_weight=query_weight, key_weight=key_weight, value_weight=value_weight, gate_weight=gate_weight, alpha_weight=alpha_weight, beta_weight=beta_weight, conv_query=conv_query, conv_key=conv_key, conv_value=conv_value, decay_log=decay_log, decay_bias=decay_bias, output_gain=output_gain, output_weight=output_weight, norm_gain_ffn=norm_gain_ffn, ffn_gate=ffn_gate, ffn_up=ffn_up, ffn_down=ffn_down, grad_block=grad_block)


highest = lax.Precision.HIGHEST
eps_norm = 1e-06
eps_output = 1e-05

def short_conv(values, kernel, segment):
    length = values.shape[0]
    result = kernel[0] * values
    for offset in range(1, kernel.shape[0]):
        before = jnp.concatenate([jnp.zeros((offset, values.shape[1]), values.dtype), values[:length - offset]], axis=0)
        earlier = jnp.concatenate([jnp.full((offset,), -1, jnp.int32), segment[:length - offset]], axis=0)
        same_doc = (segment == earlier).astype(values.dtype)[:, None]
        result = result + kernel[offset] * before * same_doc
    return result

def delta_block(carry, pieces):
    state, last_segment = carry
    query, key, value, beta, logdecay, segment = pieces
    width = segment.shape[0]
    cumul = jnp.cumsum(logdecay, axis=1)
    row_index = lax.broadcasted_iota(jnp.int32, (width, width), 0)
    col_index = lax.broadcasted_iota(jnp.int32, (width, width), 1)
    within = (segment[:, None] == segment[None, :]) & (row_index >= col_index)
    strict = within & (row_index > col_index)
    spread = cumul[:, :, None] - cumul[:, None, :]
    decay = jnp.where(within[None], jnp.exp(jnp.where(within[None], spread, 0.0)), 0.0)
    carried = jnp.where((segment == last_segment)[None, :], jnp.exp(cumul), 0.0)
    keykey = jnp.einsum('hcd,hed->hce', key, key, precision=highest)
    lower = jnp.where(strict[None], beta[:, :, None] * decay * keykey, 0.0)
    system = lower + jnp.eye(width, dtype=query.dtype)[None]
    known = jnp.einsum('hcd,hdf->hcf', key, state, precision=highest)
    target = beta[:, :, None] * (value - carried[:, :, None] * known)
    update = lax.linalg.triangular_solve(system, target, left_side=True, lower=True, unit_diagonal=True)
    scores = jnp.einsum('hcd,hed->hce', query, key, precision=highest) * decay
    output = carried[:, :, None] * jnp.einsum('hcd,hdf->hcf', query, state, precision=highest)
    output = output + jnp.einsum('hce,hef->hcf', scores, update, precision=highest)
    weighted = decay[:, -1, :][:, :, None] * key
    state = carried[:, -1][:, None, None] * state + jnp.einsum('hcd,hcf->hdf', weighted, update, precision=highest)
    return ((state, segment[-1]), output)

def mixer_core(segment, proj_q, proj_k, proj_v, proj_g, proj_a, proj_b, conv_q, conv_k, conv_v, decay_log, decay_bias, output_gain):
    length = proj_q.shape[0]
    heads = decay_log.shape[0]
    query = jax.nn.silu(short_conv(proj_q, conv_q.reshape(conv_q.shape[0], -1), segment)).reshape(length, heads, -1)
    key = jax.nn.silu(short_conv(proj_k, conv_k.reshape(conv_k.shape[0], -1), segment)).reshape(length, heads, -1)
    value = jax.nn.silu(short_conv(proj_v, conv_v.reshape(conv_v.shape[0], -1), segment)).reshape(length, heads, -1)
    query = query * lax.rsqrt(lax.optimization_barrier(jnp.sum(query * query, axis=-1, keepdims=True)) + eps_norm) * query.shape[-1] ** (-0.5)
    key = key * lax.rsqrt(lax.optimization_barrier(jnp.sum(key * key, axis=-1, keepdims=True)) + eps_norm)
    beta = jax.nn.sigmoid(proj_b)
    logdecay = -jnp.exp(decay_log) * jax.nn.softplus(proj_a + decay_bias)
    blocks = length // GROUP

    def arrange(tensor):
        return jnp.moveaxis(tensor.reshape(blocks, GROUP, heads, -1), 2, 1)

    def arrange_gate(tensor):
        return jnp.moveaxis(tensor.reshape(blocks, GROUP, heads), 2, 1)
    initial = (jnp.zeros((heads, query.shape[-1], value.shape[-1]), query.dtype), jnp.array(-1, jnp.int32))
    final, output = lax.scan(delta_block, initial, (arrange(query), arrange(key), arrange(value), arrange_gate(beta), arrange_gate(logdecay), segment.reshape(blocks, GROUP)))
    output = jnp.moveaxis(output, 1, 2).reshape(length, heads, -1)
    scale = lax.rsqrt(lax.optimization_barrier(jnp.mean(output * output, axis=-1, keepdims=True)) + eps_output)
    gated = output * scale * output_gain * jax.nn.silu(proj_g.reshape(length, heads, -1))
    return gated.reshape(length, -1)

def row_scale(values):
    return lax.rsqrt(lax.optimization_barrier(jnp.mean(values * values, axis=-1, keepdims=True)) + eps_norm)

def norm_back(grad, normed, scale):
    return scale * (grad - normed * lax.optimization_barrier(jnp.mean(grad * normed, axis=-1, keepdims=True)))

def reference(tokens, segment_ids, norm_gain_mixer, query_weight, key_weight, value_weight, gate_weight, alpha_weight, beta_weight, conv_query, conv_key, conv_value, decay_log, decay_bias, output_gain, output_weight, norm_gain_ffn, ffn_gate, ffn_up, ffn_down, grad_block):
    sequences = tokens.shape[0] // LEN
    stacked = (tokens.reshape(sequences, LEN, D), segment_ids.reshape(sequences, LEN), grad_block.reshape(sequences, LEN, D))
    shaped = (norm_gain_mixer, query_weight, key_weight, value_weight, gate_weight, alpha_weight, beta_weight, conv_query, conv_key, conv_value, decay_log, decay_bias, output_gain, output_weight, norm_gain_ffn, ffn_gate, ffn_up, ffn_down)
    initial = tuple((jnp.zeros(item.shape, jnp.float32) for item in shaped))
    gain_mix = norm_gain_mixer.astype(jnp.float32)
    gain_ffn = norm_gain_ffn.astype(jnp.float32)
    in_weights = (query_weight, key_weight, value_weight, gate_weight, alpha_weight, beta_weight)

    def one_sequence(totals, items):
        seq_tokens, seq_segments, seq_grad = items
        resid_in = seq_tokens.astype(jnp.float32)
        mixer_rms = row_scale(resid_in)
        mixer_norm = resid_in * mixer_rms
        mixer_in = (mixer_norm * gain_mix).astype(jnp.bfloat16)
        projected = [jnp.dot(mixer_in.astype(jnp.float32), weight.astype(jnp.float32), preferred_element_type=jnp.float32) for weight in in_weights]
        primals = tuple(projected) + (conv_query.astype(jnp.float32), conv_key.astype(jnp.float32), conv_value.astype(jnp.float32), decay_log, decay_bias, output_gain.astype(jnp.float32))
        gated, pullback = jax.vjp(partial(mixer_core, seq_segments), *primals)
        out_gated = gated.astype(jnp.bfloat16)
        resid = resid_in + jnp.dot(out_gated.astype(jnp.float32), output_weight.astype(jnp.float32), preferred_element_type=jnp.float32)
        ffn_rms = row_scale(resid)
        ffn_norm = resid * ffn_rms
        ffn_in = (ffn_norm * gain_ffn).astype(jnp.bfloat16)
        gate_pre = jnp.dot(ffn_in.astype(jnp.float32), ffn_gate.astype(jnp.float32), preferred_element_type=jnp.float32)
        up_pre = jnp.dot(ffn_in.astype(jnp.float32), ffn_up.astype(jnp.float32), preferred_element_type=jnp.float32)
        hidden = (jax.nn.silu(gate_pre) * up_pre).astype(jnp.bfloat16)
        block_output = (resid + jnp.dot(hidden.astype(jnp.float32), ffn_down.astype(jnp.float32), preferred_element_type=jnp.float32)).astype(jnp.bfloat16)
        d_hidden = jnp.dot(seq_grad.astype(jnp.float32), ffn_down.T.astype(jnp.float32), preferred_element_type=jnp.float32)
        sigma = jax.nn.sigmoid(gate_pre)
        d_gate = (d_hidden * up_pre * sigma * (1.0 + gate_pre * (1.0 - sigma))).astype(jnp.bfloat16)
        d_up = (d_hidden * jax.nn.silu(gate_pre)).astype(jnp.bfloat16)
        down_grad = jnp.dot(hidden.T.astype(jnp.float32), seq_grad.astype(jnp.float32), preferred_element_type=jnp.float32)
        fgate_grad = jnp.dot(ffn_in.T.astype(jnp.float32), d_gate.astype(jnp.float32), preferred_element_type=jnp.float32)
        fup_grad = jnp.dot(ffn_in.T.astype(jnp.float32), d_up.astype(jnp.float32), preferred_element_type=jnp.float32)
        d_ffn_in = jnp.dot(d_gate.astype(jnp.float32), ffn_gate.T.astype(jnp.float32), preferred_element_type=jnp.float32) + jnp.dot(d_up.astype(jnp.float32), ffn_up.T.astype(jnp.float32), preferred_element_type=jnp.float32)
        ffn_gain_grad = lax.optimization_barrier(jnp.sum(d_ffn_in * ffn_norm, axis=0))
        d_resid = seq_grad.astype(jnp.float32) + norm_back(d_ffn_in * gain_ffn, ffn_norm, ffn_rms)
        d_mix = d_resid.astype(jnp.bfloat16)
        d_gated = jnp.dot(d_mix.astype(jnp.float32), output_weight.T.astype(jnp.float32), preferred_element_type=jnp.float32)
        outweight_grad = jnp.dot(out_gated.T.astype(jnp.float32), d_mix.astype(jnp.float32), preferred_element_type=jnp.float32)
        pulled = pullback(d_gated)
        rounded = [piece.astype(jnp.bfloat16) for piece in pulled[:6]]
        proj_grads = [jnp.dot(mixer_in.T.astype(jnp.float32), piece.astype(jnp.float32), preferred_element_type=jnp.float32) for piece in rounded]
        d_mixer_in = jnp.zeros(resid_in.shape, jnp.float32)
        for piece, weight in zip(rounded, in_weights):
            d_mixer_in = d_mixer_in + jnp.dot(piece.astype(jnp.float32), weight.T.astype(jnp.float32), preferred_element_type=jnp.float32)
        mix_gain_grad = lax.optimization_barrier(jnp.sum(d_mixer_in * mixer_norm, axis=0))
        tokens_grad = d_resid + norm_back(d_mixer_in * gain_mix, mixer_norm, mixer_rms)
        grads = (mix_gain_grad,) + tuple(proj_grads) + tuple(pulled[6:12]) + (outweight_grad, ffn_gain_grad, fgate_grad, fup_grad, down_grad)
        return (tuple((total + grad for total, grad in zip(totals, grads))), (block_output, tokens_grad))
    totals, (outputs, input_grads) = lax.scan(one_sequence, initial, stacked)
    g_mix, g_query, g_key, g_value, g_gate, g_alpha, g_beta, g_convq, g_convk, g_convv, g_dlog, g_dbias, g_ogain, g_oweight, g_ffn, g_fgate, g_fup, g_fdown = totals
    return (outputs.reshape(-1, D), input_grads.reshape(-1, D), g_mix, g_query, g_key, g_value, g_gate, g_alpha, g_beta, g_convq, g_convk, g_convv, g_dlog, g_dbias, g_ogain, g_oweight, g_ffn, g_fgate, g_fup, g_fdown)
```

```python
from functools import partial

import jax
import jax.numpy as jnp
from jax import lax
from jax.experimental import pallas as pl
from jax.experimental.pallas import tpu as pltpu
from jax.sharding import PartitionSpec as P

LEN = 512
CHUNK = 128
TAPS = 4
HALO = 8
SMALL = 128

eps_norm = 1e-06
eps_output = 1e-05
EXACT = lax.Precision.HIGHEST
THREE = lax.Precision.HIGH
f32 = jnp.float32
bf16 = jnp.bfloat16


def mm(left, right, precision=None):
    return lax.dot_general(
        left, right, (((1,), (0,)), ((), ())), precision=precision, preferred_element_type=f32
    )


def mm_nt(left, right, precision=None):
    return lax.dot_general(
        left, right, (((1,), (1,)), ((), ())), precision=precision, preferred_element_type=f32
    )


def mm_tn(left, right, precision=None):
    return lax.dot_general(
        left, right, (((0,), (0,)), ((), ())), precision=precision, preferred_element_type=f32
    )


def sigmoid(value):
    return 1.0 / (1.0 + jnp.exp(-value))


def softplus(value):
    return jnp.maximum(value, 0.0) + jnp.log1p(jnp.exp(-jnp.abs(value)))


def iotas(size):
    row = lax.broadcasted_iota(jnp.int32, (size, size), 0)
    col = lax.broadcasted_iota(jnp.int32, (size, size), 1)
    return row, col


def conv_taps(block, before, meta, taps):
    size = block.shape[0]
    joined = jnp.concatenate([before, block], axis=0)
    total = taps[0:1] * block
    shifted = []
    for offset in range(1, TAPS):
        moved = joined[HALO - offset : HALO - offset + size] * meta[:, offset : offset + 1]
        shifted.append(moved)
        total = total + taps[offset : offset + 1] * moved
    return total, shifted


def gates(small, head, heads, decay_log, decay_bias):
    pre_a = small[:, head : head + 1] + decay_bias[:, head : head + 1]
    beta = sigmoid(small[:, heads + head : heads + head + 1])
    rate = -jnp.exp(decay_log[:, head : head + 1])
    return pre_a, beta, rate, rate * softplus(pre_a)


def decays(logdecay, meta, seg_row, row, col):
    size = logdecay.shape[0]
    within = (meta[:, 0:1] == seg_row) & (row >= col)
    ones_below = (row >= col).astype(f32)
    cumul = mm(ones_below, jnp.broadcast_to(logdecay, (size, size)), EXACT)
    spread = cumul - cumul.T
    decay = jnp.where(within, jnp.exp(jnp.where(within, spread, 0.0)), 0.0)
    carried = jnp.where(meta[:, 4:5] > 0.0, jnp.exp(cumul), 0.0)
    stays = meta[:, 0:1] == seg_row[:, size - 1 : size]
    weight = jnp.where(stays, jnp.exp(jnp.where(stays, cumul[size - 1 : size] - cumul, 0.0)), 0.0)
    return within, decay, carried, weight


def unit_inverse(lowers, row, col, precision):
    size = lowers[0].shape[0]
    eye = (row == col).astype(f32)
    base = 8
    same = (row // base) == (col // base)
    inner = [jnp.where(same, lower, 0.0) for lower in lowers]
    second = [mm(item, item, precision) for item in inner]
    fourth = [mm(item, item, precision) for item in second]
    inverse = [eye - item for item in inner]
    inverse = [item + mm(item, power, precision) for item, power in zip(inverse, second)]
    inverse = [item + mm(item, power, precision) for item, power in zip(inverse, fourth)]
    while base < size:
        joined = ((row // (2 * base)) == (col // (2 * base))) & ((row // base) != (col // base))
        outer = [jnp.where(joined, lower, 0.0) for lower in lowers]
        step = [mm(item, part, precision) for item, part in zip(inverse, outer)]
        step = [mm(item, part, precision) for item, part in zip(step, inverse)]
        inverse = [item - part for item, part in zip(inverse, step)]
        base = 2 * base
    return inverse


def mixer_forward_kernel(
    heads,
    width_k,
    width_v,
    proj,
    meta_ref,
    seg_ref,
    taps_ref,
    scalars_ref,
    gain_ref,
    gated_ref,
    raw_ref,
    update_ref,
    inverse_ref,
    state_ref,
    state,
    tail,
):
    step = pl.program_id(0)
    size = proj.shape[0]
    mixed = heads * (2 * width_k + width_v)
    small_at = mixed + heads * width_v

    @pl.when(step == 0)
    def _():
        state[...] = jnp.zeros_like(state)
        tail[...] = jnp.zeros_like(tail)

    meta = meta_ref[...]
    seg_row = seg_ref[0:1, :]
    decay_log = scalars_ref[0:1, :]
    decay_bias = scalars_ref[1:2, :]
    small = proj[:, small_at : small_at + SMALL]
    row, col = iotas(size)
    total, _ = conv_taps(proj[:, :mixed], tail[...], meta, taps_ref[...])
    tail[...] = proj[size - HALO : size, :mixed]
    active = total * sigmoid(total)
    queries, keys, values, betas, carries, weights, scores, lowers = [], [], [], [], [], [], [], []
    for head in range(heads):
        query = active[:, head * width_k : (head + 1) * width_k]
        query = query * (
            lax.rsqrt(jnp.sum(query * query, axis=1, keepdims=True) + eps_norm) * width_k**-0.5
        )
        key_at = heads * width_k + head * width_k
        key = active[:, key_at : key_at + width_k]
        key = key * lax.rsqrt(jnp.sum(key * key, axis=1, keepdims=True) + eps_norm)
        value_at = 2 * heads * width_k + head * width_v
        value = active[:, value_at : value_at + width_v]
        _, beta, _, logdecay = gates(small, head, heads, decay_log, decay_bias)
        within, decay, carried, weight = decays(logdecay, meta, seg_row, row, col)
        lower = jnp.where(row > col, beta * decay * mm_nt(key, key, THREE), 0.0)
        queries.append(query)
        keys.append(key)
        values.append(value)
        betas.append(beta)
        carries.append(carried)
        weights.append(weight)
        scores.append(mm_nt(query, key, THREE) * decay)
        lowers.append(lower)
    inverses = unit_inverse(lowers, row, col, THREE)
    for head in range(heads):
        entry = state[head]
        carried = carries[head]
        wide = jnp.concatenate([carried] * (width_v // size), axis=1)
        known = mm(keys[head], entry, THREE)
        target = betas[head] * (values[head] - wide * known)
        update = mm(inverses[head], target, THREE)
        output = wide * mm(queries[head], entry, THREE) + mm(scores[head], update, THREE)
        state_ref[0, head] = entry
        inverse_ref[0, head] = inverses[head]
        state[head] = wide[size - 1 : size] * entry + mm_tn(
            weights[head] * keys[head], update, THREE
        )
        span = slice(head * width_v, (head + 1) * width_v)
        update_ref[:, span] = update
        raw_ref[:, span] = output
        scale = lax.rsqrt(jnp.mean(output * output, axis=1, keepdims=True) + eps_output)
        pre = proj[:, mixed + head * width_v : mixed + (head + 1) * width_v]
        gated = output * scale * gain_ref[0:1, span] * (pre * sigmoid(pre))
        gated_ref[:, span] = gated.astype(bf16)


def mixer_backward_kernel(
    heads,
    width_k,
    width_v,
    proj,
    before_ref,
    meta_ref,
    seg_ref,
    taps_ref,
    scalars_ref,
    gain_ref,
    d_gated_ref,
    raw_ref,
    update_ref,
    inverse_ref,
    state_ref,
    d_proj_ref,
    d_taps_ref,
    d_gain_ref,
    d_scalars_ref,
    d_state,
    ahead,
):
    step = pl.program_id(0)
    size = proj.shape[0]
    mixed = heads * (2 * width_k + width_v)
    small_at = mixed + heads * width_v

    @pl.when(step == 0)
    def _():
        d_state[...] = jnp.zeros_like(d_state)
        ahead[...] = jnp.zeros_like(ahead)
        d_taps_ref[...] = jnp.zeros_like(d_taps_ref)
        d_gain_ref[...] = jnp.zeros_like(d_gain_ref)
        d_scalars_ref[...] = jnp.zeros_like(d_scalars_ref)

    meta = meta_ref[...]
    seg_row = seg_ref[0:1, :]
    decay_log = scalars_ref[0:1, :]
    decay_bias = scalars_ref[1:2, :]
    taps = taps_ref[...]
    small = proj[:, small_at : small_at + SMALL]
    row, col = iotas(size)
    block = proj[:, :mixed]
    total, shifted = conv_taps(block, before_ref[:, :mixed], meta, taps)
    gate = sigmoid(total)
    active = total * gate
    lane = lax.broadcasted_iota(jnp.int32, (size, SMALL), 1)
    small_grad = jnp.zeros((size, SMALL), f32)
    d_query_parts, d_key_parts, d_value_parts = [], [], []
    for head in range(heads):
        span = slice(head * width_v, (head + 1) * width_v)
        query_raw = active[:, head * width_k : (head + 1) * width_k]
        query_scale = lax.rsqrt(jnp.sum(query_raw * query_raw, axis=1, keepdims=True) + eps_norm)
        query_unit = query_raw * query_scale
        query = query_unit * width_k**-0.5
        key_at = heads * width_k + head * width_k
        key_raw = active[:, key_at : key_at + width_k]
        key_scale = lax.rsqrt(jnp.sum(key_raw * key_raw, axis=1, keepdims=True) + eps_norm)
        key = key_raw * key_scale
        value_at = 2 * heads * width_k + head * width_v
        value = active[:, value_at : value_at + width_v]
        pre_a, beta, rate, logdecay = gates(small, head, heads, decay_log, decay_bias)
        within, decay, carried, weight = decays(logdecay, meta, seg_row, row, col)
        wide = jnp.concatenate([carried] * (width_v // size), axis=1)
        keyed = decay * mm_nt(key, key, THREE)
        keyed = jnp.where(row > col, keyed, 0.0)
        scores = mm_nt(query, key, THREE) * decay
        entry = state_ref[0, head]
        inverse = inverse_ref[0, head]
        update = update_ref[:, span]
        output = raw_ref[:, span]
        scale = lax.rsqrt(jnp.mean(output * output, axis=1, keepdims=True) + eps_output)
        normed = output * scale
        pre = proj[:, mixed + head * width_v : mixed + (head + 1) * width_v]
        pre_gate = sigmoid(pre)
        silu = pre * pre_gate
        gain = gain_ref[0:1, span]
        d_gated = d_gated_ref[:, span]
        gained = d_gated * normed
        d_gain_ref[0:1, span] += jnp.sum(gained * silu, axis=0, keepdims=True)
        d_pre = gained * gain * (pre_gate * (1.0 + pre * (1.0 - pre_gate)))
        d_proj_ref[:, mixed + head * width_v : mixed + (head + 1) * width_v] = d_pre.astype(bf16)
        d_normed = d_gated * gain * silu
        d_output = scale * (
            d_normed - normed * jnp.mean(d_normed * normed, axis=1, keepdims=True)
        )
        d_exit = d_state[head]
        weighted = weight * key
        d_update = mm_tn(scores, d_output, THREE) + mm(weighted, d_exit, THREE)
        d_target = mm_tn(inverse, d_update, THREE)
        d_lower = jnp.where(row > col, -mm_nt(d_target, update, THREE), 0.0)
        d_scores = mm_nt(d_output, update, THREE)
        from_output = mm_nt(d_output, entry, THREE)
        from_target = mm_nt(d_target, entry, THREE)
        from_exit = mm_nt(update, d_exit, THREE)
        d_inner = d_scores * decay
        pair = d_lower * beta * decay
        d_query = carried * from_output + mm(d_inner, key, THREE)
        d_key = (
            mm_tn(d_inner, query, THREE)
            + weight * from_exit
            + mm(pair + pair.T, key, THREE)
            - beta * carried * from_target
        )
        d_value = beta * d_target
        d_state[head] = (
            wide[size - 1 : size] * d_exit
            + mm_tn(query, wide * d_output, THREE)
            - mm_tn(key, wide * d_value, THREE)
        )
        known_part = jnp.sum(key * from_target, axis=1, keepdims=True)
        carried_col = carried[:, 0:1]
        d_beta = (
            jnp.sum(d_target * value, axis=1, keepdims=True)
            - carried_col * known_part
            + jnp.sum(d_lower * keyed, axis=1, keepdims=True)
        )
        d_carried = jnp.sum(query * from_output, axis=1, keepdims=True) - beta * known_part
        d_spread = d_scores * scores + d_lower * (beta * keyed)
        d_weight = jnp.sum(weighted * from_exit, axis=1, keepdims=True)
        last = (row[:, 0:1] == size - 1).astype(f32)
        at_last = jnp.sum(d_weight, axis=0, keepdims=True) + carried_col[
            size - 1 : size
        ] * jnp.sum(jnp.sum(d_exit * entry, axis=1, keepdims=True), axis=0, keepdims=True)
        d_cumul = (
            jnp.sum(d_spread - d_spread.T, axis=1, keepdims=True)
            + d_carried * carried_col
            - d_weight
            + last * at_last
        )
        ones_above = (row <= col).astype(f32)
        d_logdecay = mm(ones_above, jnp.broadcast_to(d_cumul, (size, size)), EXACT)[:, 0:1]
        d_alpha = d_logdecay * rate * sigmoid(pre_a)
        d_scalars_ref[0:1, head : head + 1] += jnp.sum(
            d_logdecay * logdecay, axis=0, keepdims=True
        )
        d_scalars_ref[1:2, head : head + 1] += jnp.sum(d_alpha, axis=0, keepdims=True)
        small_grad = jnp.where(lane == head, d_alpha, small_grad)
        small_grad = jnp.where(lane == heads + head, d_beta * beta * (1.0 - beta), small_grad)
        d_query = d_query * width_k**-0.5
        d_query_parts.append(
            query_scale
            * (d_query - query_unit * jnp.sum(d_query * query_unit, axis=1, keepdims=True))
        )
        d_key_parts.append(key_scale * (d_key - key * jnp.sum(d_key * key, axis=1, keepdims=True)))
        d_value_parts.append(d_value)
    d_proj_ref[:, small_at : small_at + SMALL] = small_grad.astype(bf16)
    d_active = jnp.concatenate(d_query_parts + d_key_parts + d_value_parts, axis=1)
    d_total = d_active * (gate * (1.0 + total * (1.0 - gate)))
    d_block = taps[0:1] * d_total
    d_taps_ref[0:1, :] += jnp.sum(d_total * block, axis=0, keepdims=True)
    for offset in range(1, TAPS):
        d_taps_ref[offset : offset + 1, :] += jnp.sum(
            d_total * shifted[offset - 1], axis=0, keepdims=True
        )
        masked = d_total * meta[:, offset : offset + 1]
        joined = jnp.concatenate([masked, ahead[offset]], axis=0)
        d_block = d_block + taps[offset : offset + 1] * joined[offset : offset + size]
        ahead[offset] = masked[:HALO]
    d_proj_ref[:, :mixed] = d_block.astype(bf16)


def mixer_forward(proj, meta, seg_rows, taps, scalars, gain, heads, width_k, width_v):
    length = proj.shape[0]
    chunks = length // CHUNK
    mixed = heads * (2 * width_k + width_v)
    whole = lambda shape: pl.BlockSpec(shape, lambda c: (0,) * len(shape))
    rows = lambda width: pl.BlockSpec((CHUNK, width), lambda c: (c, 0))
    block4 = lambda a, b: pl.BlockSpec((1, heads, a, b), lambda c: (c, 0, 0, 0))
    return pl.pallas_call(
        partial(mixer_forward_kernel, heads, width_k, width_v),
        grid=(chunks,),
        in_specs=[
            rows(proj.shape[1]),
            rows(SMALL),
            pl.BlockSpec((8, CHUNK), lambda c: (c, 0)),
            whole(taps.shape),
            whole(scalars.shape),
            whole(gain.shape),
        ],
        out_specs=[
            rows(heads * width_v),
            rows(heads * width_v),
            rows(heads * width_v),
            block4(CHUNK, CHUNK),
            block4(width_k, width_v),
        ],
        out_shape=[
            jax.ShapeDtypeStruct((length, heads * width_v), bf16),
            jax.ShapeDtypeStruct((length, heads * width_v), f32),
            jax.ShapeDtypeStruct((length, heads * width_v), f32),
            jax.ShapeDtypeStruct((chunks, heads, CHUNK, CHUNK), f32),
            jax.ShapeDtypeStruct((chunks, heads, width_k, width_v), f32),
        ],
        scratch_shapes=[
            pltpu.VMEM((heads, width_k, width_v), f32),
            pltpu.VMEM((HALO, mixed), f32),
        ],
        name="mixer_forward",
    )(proj, meta, seg_rows, taps, scalars, gain)


def mixer_backward(
    proj, meta, seg_rows, taps, scalars, gain, d_gated, saved, heads, width_k, width_v
):
    length = proj.shape[0]
    chunks = length // CHUNK
    mixed = heads * (2 * width_k + width_v)
    last = chunks - 1
    per = CHUNK // HALO
    whole = lambda shape: pl.BlockSpec(shape, lambda c: (0,) * len(shape))
    rows = lambda width: pl.BlockSpec((CHUNK, width), lambda c: (last - c, 0))
    block4 = lambda a, b: pl.BlockSpec((1, heads, a, b), lambda c: (last - c, 0, 0, 0))
    raw, update, inverse, state = saved
    return pl.pallas_call(
        partial(mixer_backward_kernel, heads, width_k, width_v),
        grid=(chunks,),
        in_specs=[
            rows(proj.shape[1]),
            pl.BlockSpec(
                (HALO, proj.shape[1]), lambda c: (jnp.maximum((last - c) * per - 1, 0), 0)
            ),
            rows(SMALL),
            pl.BlockSpec((8, CHUNK), lambda c: (last - c, 0)),
            whole(taps.shape),
            whole(scalars.shape),
            whole(gain.shape),
            rows(heads * width_v),
            rows(heads * width_v),
            rows(heads * width_v),
            block4(CHUNK, CHUNK),
            block4(width_k, width_v),
        ],
        out_specs=[
            rows(proj.shape[1]),
            whole((8, mixed)),
            whole((8, heads * width_v)),
            whole((8, SMALL)),
        ],
        out_shape=[
            jax.ShapeDtypeStruct(proj.shape, bf16),
            jax.ShapeDtypeStruct((8, mixed), f32),
            jax.ShapeDtypeStruct((8, heads * width_v), f32),
            jax.ShapeDtypeStruct((8, SMALL), f32),
        ],
        scratch_shapes=[
            pltpu.VMEM((heads, width_k, width_v), f32),
            pltpu.VMEM((TAPS, HALO, mixed), f32),
        ],
        name="mixer_backward",
    )(proj, proj, meta, seg_rows, taps, scalars, gain, d_gated, raw, update, inverse, state)


def segment_tables(segment):
    length = segment.shape[0]
    columns = [segment.astype(f32)]
    for offset in range(1, TAPS):
        earlier = jnp.concatenate([jnp.full((offset,), -1, jnp.int32), segment[: length - offset]])
        columns.append((segment == earlier).astype(f32))
    ends = segment.reshape(-1, CHUNK)[:, -1]
    ends = jnp.concatenate([jnp.full((1,), -1, jnp.int32), ends[:-1]])
    columns.append((segment == jnp.repeat(ends, CHUNK)).astype(f32))
    meta = jnp.stack(columns, axis=1)
    meta = jnp.pad(meta, ((0, 0), (0, SMALL - meta.shape[1])))
    seg_rows = jnp.repeat(segment.astype(f32).reshape(-1, 1, CHUNK), 8, axis=1).reshape(-1, CHUNK)
    return meta, seg_rows


def row_scale(values):
    return lax.rsqrt(jnp.mean(values * values, axis=-1, keepdims=True) + eps_norm)


def norm_back(grad, normed, scale):
    return scale * (grad - normed * jnp.mean(grad * normed, axis=-1, keepdims=True))


def swap_core(value, axis, size):
    return lax.ppermute(value, axis, [(i, i ^ 1) for i in range(size)])


def swap_chip(value, axis, size):
    return lax.ppermute(value, axis, [(i, i ^ 2) for i in range(size)])


def pick(stacked, index, dim):
    return lax.dynamic_index_in_dim(stacked, index, dim, keepdims=False)


def interleave(mine, other, index, dim):
    first = index == 0
    return jnp.stack([jnp.where(first, mine, other), jnp.where(first, other, mine)], axis=dim)


def gather_rows(block, axis, size, chip, core):
    over = swap_chip(block, axis, size)
    pair = interleave(block, over, chip, 0)
    other = swap_core(pair, axis, size)
    return interleave(pair, other, core, 1).reshape(size * block.shape[0], block.shape[1])


def core_sum(partial_rows, axis, size, core):
    rows = partial_rows.shape[0] // size
    parts = partial_rows.reshape(2, 2, rows, partial_rows.shape[1])
    return pick(parts, core, 1) + swap_core(pick(parts, 1 - core, 1), axis, size)


def reduce_half(partial_rows, axis, size, core):
    mine = core_sum(partial_rows, axis, size, core).astype(bf16)
    return mine.astype(f32) + swap_chip(mine, axis, size).astype(f32)


def reduce_own(partial_rows, axis, size, chip, core):
    mine = core_sum(partial_rows, axis, size, core)
    away = swap_chip(pick(mine, 1 - chip, 0).astype(bf16), axis, size)
    return pick(mine, chip, 0) + away.astype(f32)


def join_halves(half, axis, size, core):
    other = swap_core(half, axis, size)
    return interleave(half, other, core, 1).reshape(-1, half.shape[-1])


def per_device(
    tokens,
    segment_ids,
    norm_gain_mixer,
    query_weight,
    key_weight,
    value_weight,
    gate_weight,
    alpha_weight,
    beta_weight,
    conv_query,
    conv_key,
    conv_value,
    decay_log,
    decay_bias,
    output_gain,
    output_weight,
    norm_gain_ffn,
    ffn_gate,
    ffn_up,
    ffn_down,
    grad_block,
):
    n_dp = lax.axis_size("dp")
    n_t = lax.axis_size("tensor")
    place = lax.axis_index("tensor")
    chip, core = place // 2, place % 2
    rows, width = tokens.shape
    owned = query_weight.shape[0]
    heads = decay_log.shape[0]
    width_k = query_weight.shape[1] // heads
    width_v = value_weight.shape[1] // heads
    hidden_units = ffn_gate.shape[1]
    mixed = heads * (2 * width_k + width_v)
    inner = heads * width_v
    gather_weights = lambda block: lax.all_gather(block, "dp", axis=0, tiled=True)

    thin = [
        alpha_weight,
        beta_weight,
        norm_gain_mixer.reshape(owned, 1),
        norm_gain_ffn.reshape(owned, 1),
        conv_query.reshape(owned, -1),
        conv_key.reshape(owned, -1),
        conv_value.reshape(owned, -1),
        jnp.pad(output_gain.reshape(-1), (0, owned - output_gain.size)).reshape(owned, 1),
    ]
    thin = jnp.concatenate(thin, axis=1)
    thin = jnp.pad(thin, ((0, 0), (0, SMALL - thin.shape[1])))
    weights = gather_weights(
        jnp.concatenate([query_weight, key_weight, value_weight, gate_weight, thin], axis=1)
    )
    later = gather_weights(
        jnp.concatenate([ffn_gate, ffn_up, ffn_down.T, output_weight.T], axis=1)
    )
    gate_up = later[:, : 2 * hidden_units]
    down_t = later[:, 2 * hidden_units : 3 * hidden_units]
    out_t = later[:, 3 * hidden_units :]

    tokens_full = gather_rows(tokens, "tensor", n_t, chip, core)
    grad_full = gather_rows(grad_block, "tensor", n_t, chip, core)

    thin_t = weights[:, mixed + inner :].astype(f32).T
    gain_mix = thin_t[2 * heads : 2 * heads + 1]
    gain_ffn = thin_t[2 * heads + 1 : 2 * heads + 2]

    def taps_of(first, count, size):
        flat = thin_t[first : first + count].T
        return flat.reshape(n_dp, TAPS, heads, size // n_dp).transpose(1, 2, 0, 3).reshape(TAPS, -1)

    at = 2 * heads + 2
    taps = jnp.concatenate(
        [taps_of(at, 1, width_k), taps_of(at + 1, 1, width_k), taps_of(at + 2, 2, width_v)], axis=1
    )
    taps = jnp.pad(taps, ((0, 8 - TAPS), (0, 0)))
    out_gain = thin_t[at + 4].reshape(n_dp, owned)[:, : output_gain.size]
    out_gain = out_gain.reshape(n_dp, heads, width_v // n_dp).transpose(1, 0, 2).reshape(1, inner)
    out_gain = jnp.pad(out_gain, ((0, 7), (0, 0)))
    scalars = jnp.pad(jnp.stack([decay_log, decay_bias]), ((0, 6), (0, SMALL - heads)))
    meta, seg_rows = segment_tables(segment_ids)

    resid_in = tokens_full.astype(f32)
    mixer_norm = resid_in * row_scale(resid_in)
    mixer_in = (mixer_norm * gain_mix).astype(bf16)
    proj = mm(mixer_in, weights)
    sizes = (heads, width_k, width_v)
    out_gated, *saved = mixer_forward(proj, meta, seg_rows, taps, scalars, out_gain, *sizes)
    mixer_out = reduce_half(mm_nt(out_gated, out_t), "tensor", n_t, core)

    def half_of(full):
        return pick(full.reshape(2, 2, rows, width), core, 1)

    resid = half_of(tokens_full).astype(f32) + mixer_out
    ffn_rms = row_scale(resid)
    ffn_norm = resid * ffn_rms
    ffn_in = join_halves((ffn_norm * gain_ffn).astype(bf16), "tensor", n_t, core)

    pre = mm(ffn_in, gate_up)
    gate_pre, up_pre = pre[:, :hidden_units], pre[:, hidden_units:]
    sigma = jax.nn.sigmoid(gate_pre)
    silu = gate_pre * sigma
    hidden = (silu * up_pre).astype(bf16)
    d_hidden = mm(grad_full, down_t)
    d_gate = d_hidden * up_pre * sigma * (1.0 + gate_pre * (1.0 - sigma))
    d_pre = jnp.concatenate([d_gate.astype(bf16), (d_hidden * silu).astype(bf16)], axis=1)
    d_ffn_in = reduce_half(mm_nt(d_pre, gate_up), "tensor", n_t, core)
    d_resid = half_of(grad_full).astype(f32) + norm_back(d_ffn_in * gain_ffn, ffn_norm, ffn_rms)
    d_mix = join_halves(d_resid.astype(bf16), "tensor", n_t, core)
    ffn_out = reduce_own(mm_nt(hidden, down_t), "tensor", n_t, chip, core)
    block_output = (pick(resid, chip, 0) + ffn_out).astype(bf16)
    ffn_gain_part = jnp.sum(pick(d_ffn_in * ffn_norm, chip, 0), axis=0)

    def scatter(blocks):
        joined = jnp.concatenate([block.astype(bf16) for block in blocks], axis=1)
        return lax.psum_scatter(joined, "dp", scatter_dimension=0, tiled=True).astype(f32)

    ffn_grads = scatter([mm_tn(ffn_in, d_pre), mm_tn(grad_full, hidden)])

    d_gated = mm(d_mix, out_t)
    d_proj, d_taps, d_gain, d_scalars = mixer_backward(
        proj, meta, seg_rows, taps, scalars, out_gain, d_gated, saved, *sizes
    )
    mixer_grads = scatter([mm_tn(d_mix, out_gated), mm_tn(mixer_in, d_proj)])
    d_mixer_in = reduce_own(mm_nt(d_proj, weights), "tensor", n_t, chip, core)
    own_tokens = tokens.astype(f32)
    own_rms = row_scale(own_tokens)
    own_norm = own_tokens * own_rms
    mix_gain_part = jnp.sum(d_mixer_in * own_norm, axis=0)
    tokens_grad = pick(d_resid, chip, 0) + norm_back(d_mixer_in * gain_mix, own_norm, own_rms)

    gain_sums = lax.psum((mix_gain_part, ffn_gain_part), ("dp", "tensor"))
    head_sums = lax.psum((d_taps[:TAPS], d_gain[0], d_scalars[:2, :heads]), "dp")
    dp_place = lax.axis_index("dp")
    mix_gain_grad, ffn_gain_grad = (
        lax.dynamic_slice_in_dim(part, dp_place * owned, owned, 0) for part in gain_sums
    )

    def own_columns(part, size):
        split = part.reshape(-1, heads, n_dp, size // n_dp)
        return lax.dynamic_index_in_dim(split, dp_place, 2, keepdims=False)

    taps_grad, gain_grad, scalars_grad = head_sums
    key_at, value_at = heads * width_k, 2 * heads * width_k
    conv_grads = (
        own_columns(taps_grad[:, :key_at], width_k),
        own_columns(taps_grad[:, key_at:value_at], width_k),
        own_columns(taps_grad[:, value_at:], width_v),
    )
    projected = mixer_grads[:, inner:]
    return (
        block_output,
        tokens_grad,
        mix_gain_grad,
        projected[:, :key_at],
        projected[:, key_at:value_at],
        projected[:, value_at:mixed],
        projected[:, mixed : mixed + inner],
        projected[:, mixed + inner : mixed + inner + heads],
        projected[:, mixed + inner + heads : mixed + inner + 2 * heads],
        *conv_grads,
        scalars_grad[0],
        scalars_grad[1],
        own_columns(gain_grad.reshape(1, -1), width_v)[0],
        mixer_grads[:, :inner].T,
        ffn_gain_grad,
        ffn_grads[:, :hidden_units],
        ffn_grads[:, hidden_units : 2 * hidden_units],
        ffn_grads[:, 2 * hidden_units :].T,
    )


def solution(mesh):
    by_rows = P(("dp", "tensor"), None)
    tiled, turned = P("dp", "tensor"), P("tensor", "dp")
    conv = P(None, "tensor", "dp")
    weights_in = (tiled,) * 6
    return jax.shard_map(
        per_device,
        mesh=mesh,
        in_specs=(
            by_rows,
            P("dp"),
            P("dp"),
            *weights_in,
            conv,
            conv,
            conv,
            P("tensor"),
            P("tensor"),
            turned,
            turned,
            P("dp"),
            tiled,
            tiled,
            turned,
            by_rows,
        ),
        out_specs=(
            by_rows,
            by_rows,
            P("dp"),
            *weights_in,
            conv,
            conv,
            conv,
            P("tensor"),
            P("tensor"),
            turned,
            turned,
            P("dp"),
            tiled,
            tiled,
            turned,
        ),
        check_vma=False,
    )
```

```python
from functools import partial

import jax
import jax.numpy as jnp
from jax import lax
from jax.experimental import pallas as pl
from jax.experimental.pallas import tpu as pltpu
from jax.sharding import PartitionSpec as P

LEN = 512
CHUNK = 128
TAPS = 4
HALO = 8
SMALL = 128
RING_MOST = 8

eps_norm = 1e-06
eps_output = 1e-05
EXACT = lax.Precision.HIGHEST
THREE = lax.Precision.HIGH
f32 = jnp.float32
bf16 = jnp.bfloat16


def mm(left, right, precision=None):
    return lax.dot_general(
        left, right, (((1,), (0,)), ((), ())), precision=precision, preferred_element_type=f32
    )


def mm_nt(left, right, precision=None):
    return lax.dot_general(
        left, right, (((1,), (1,)), ((), ())), precision=precision, preferred_element_type=f32
    )


def mm_tn(left, right, precision=None):
    return lax.dot_general(
        left, right, (((0,), (0,)), ((), ())), precision=precision, preferred_element_type=f32
    )


def sigmoid(value):
    return 1.0 / (1.0 + jnp.exp(-value))


def softplus(value):
    return jnp.maximum(value, 0.0) + jnp.log1p(jnp.exp(-jnp.abs(value)))


def iotas(size):
    row = lax.broadcasted_iota(jnp.int32, (size, size), 0)
    col = lax.broadcasted_iota(jnp.int32, (size, size), 1)
    return row, col


def conv_taps(block, before, meta, taps):
    size = block.shape[0]
    joined = jnp.concatenate([before, block], axis=0)
    total = taps[0:1] * block
    shifted = []
    for offset in range(1, TAPS):
        moved = joined[HALO - offset : HALO - offset + size] * meta[:, offset : offset + 1]
        shifted.append(moved)
        total = total + taps[offset : offset + 1] * moved
    return total, shifted


def gates(small, head, heads, decay_log, decay_bias):
    pre_a = small[:, head : head + 1] + decay_bias[:, head : head + 1]
    beta = sigmoid(small[:, heads + head : heads + head + 1])
    rate = -jnp.exp(decay_log[:, head : head + 1])
    return pre_a, beta, rate, rate * softplus(pre_a)


def decays(logdecay, meta, seg_row, row, col):
    size = logdecay.shape[0]
    within = (meta[:, 0:1] == seg_row) & (row >= col)
    ones_below = (row >= col).astype(f32)
    cumul = mm(ones_below, jnp.broadcast_to(logdecay, (size, size)), EXACT)
    spread = cumul - cumul.T
    decay = jnp.where(within, jnp.exp(jnp.where(within, spread, 0.0)), 0.0)
    carried = jnp.where(meta[:, 4:5] > 0.0, jnp.exp(cumul), 0.0)
    stays = meta[:, 0:1] == seg_row[:, size - 1 : size]
    weight = jnp.where(stays, jnp.exp(jnp.where(stays, cumul[size - 1 : size] - cumul, 0.0)), 0.0)
    return within, decay, carried, weight


def unit_inverse(lowers, row, col, precision):
    size = lowers[0].shape[0]
    eye = (row == col).astype(f32)
    base = 8
    same = (row // base) == (col // base)
    inner = [jnp.where(same, lower, 0.0) for lower in lowers]
    second = [mm(item, item, precision) for item in inner]
    fourth = [mm(item, item, precision) for item in second]
    inverse = [eye - item for item in inner]
    inverse = [item + mm(item, power, precision) for item, power in zip(inverse, second)]
    inverse = [item + mm(item, power, precision) for item, power in zip(inverse, fourth)]
    while base < size:
        joined = ((row // (2 * base)) == (col // (2 * base))) & ((row // base) != (col // base))
        outer = [jnp.where(joined, lower, 0.0) for lower in lowers]
        step = [mm(item, part, precision) for item, part in zip(inverse, outer)]
        step = [mm(item, part, precision) for item, part in zip(step, inverse)]
        inverse = [item - part for item, part in zip(inverse, step)]
        base = 2 * base
    return inverse


def mixer_forward_kernel(
    heads,
    width_k,
    width_v,
    proj,
    meta_ref,
    seg_ref,
    taps_ref,
    scalars_ref,
    gain_ref,
    gated_ref,
    raw_ref,
    update_ref,
    inverse_ref,
    state_ref,
    state,
    tail,
):
    step = pl.program_id(0)
    size = proj.shape[0]
    mixed = heads * (2 * width_k + width_v)
    small_at = mixed + heads * width_v

    @pl.when(step == 0)
    def _():
        state[...] = jnp.zeros_like(state)
        tail[...] = jnp.zeros_like(tail)

    meta = meta_ref[...]
    seg_row = seg_ref[0:1, :]
    decay_log = scalars_ref[0:1, :]
    decay_bias = scalars_ref[1:2, :]
    small = proj[:, small_at : small_at + SMALL]
    row, col = iotas(size)
    total, _ = conv_taps(proj[:, :mixed], tail[...], meta, taps_ref[...])
    tail[...] = proj[size - HALO : size, :mixed]
    active = total * sigmoid(total)
    queries, keys, values, betas, carries, weights, scores, lowers = [], [], [], [], [], [], [], []
    for head in range(heads):
        query = active[:, head * width_k : (head + 1) * width_k]
        query = query * (
            lax.rsqrt(jnp.sum(query * query, axis=1, keepdims=True) + eps_norm) * width_k**-0.5
        )
        key_at = heads * width_k + head * width_k
        key = active[:, key_at : key_at + width_k]
        key = key * lax.rsqrt(jnp.sum(key * key, axis=1, keepdims=True) + eps_norm)
        value_at = 2 * heads * width_k + head * width_v
        value = active[:, value_at : value_at + width_v]
        _, beta, _, logdecay = gates(small, head, heads, decay_log, decay_bias)
        within, decay, carried, weight = decays(logdecay, meta, seg_row, row, col)
        lower = jnp.where(row > col, beta * decay * mm_nt(key, key, THREE), 0.0)
        queries.append(query)
        keys.append(key)
        values.append(value)
        betas.append(beta)
        carries.append(carried)
        weights.append(weight)
        scores.append(mm_nt(query, key, THREE) * decay)
        lowers.append(lower)
    inverses = unit_inverse(lowers, row, col, THREE)
    for head in range(heads):
        entry = state[head]
        carried = carries[head]
        wide = jnp.concatenate([carried] * (width_v // size), axis=1)
        known = mm(keys[head], entry, THREE)
        target = betas[head] * (values[head] - wide * known)
        update = mm(inverses[head], target, THREE)
        output = wide * mm(queries[head], entry, THREE) + mm(scores[head], update, THREE)
        state_ref[0, head] = entry
        inverse_ref[0, head] = inverses[head]
        state[head] = wide[size - 1 : size] * entry + mm_tn(
            weights[head] * keys[head], update, THREE
        )
        span = slice(head * width_v, (head + 1) * width_v)
        update_ref[:, span] = update
        raw_ref[:, span] = output
        scale = lax.rsqrt(jnp.mean(output * output, axis=1, keepdims=True) + eps_output)
        pre = proj[:, mixed + head * width_v : mixed + (head + 1) * width_v]
        gated = output * scale * gain_ref[0:1, span] * (pre * sigmoid(pre))
        gated_ref[:, span] = gated.astype(bf16)


def mixer_backward_kernel(
    heads,
    width_k,
    width_v,
    proj,
    before_ref,
    meta_ref,
    seg_ref,
    taps_ref,
    scalars_ref,
    gain_ref,
    d_gated_ref,
    raw_ref,
    update_ref,
    inverse_ref,
    state_ref,
    d_proj_ref,
    d_taps_ref,
    d_gain_ref,
    d_scalars_ref,
    d_state,
    ahead,
):
    step = pl.program_id(0)
    size = proj.shape[0]
    mixed = heads * (2 * width_k + width_v)
    small_at = mixed + heads * width_v

    @pl.when(step == 0)
    def _():
        d_state[...] = jnp.zeros_like(d_state)
        ahead[...] = jnp.zeros_like(ahead)
        d_taps_ref[...] = jnp.zeros_like(d_taps_ref)
        d_gain_ref[...] = jnp.zeros_like(d_gain_ref)
        d_scalars_ref[...] = jnp.zeros_like(d_scalars_ref)

    meta = meta_ref[...]
    seg_row = seg_ref[0:1, :]
    decay_log = scalars_ref[0:1, :]
    decay_bias = scalars_ref[1:2, :]
    taps = taps_ref[...]
    small = proj[:, small_at : small_at + SMALL]
    row, col = iotas(size)
    block = proj[:, :mixed]
    total, shifted = conv_taps(block, before_ref[:, :mixed], meta, taps)
    gate = sigmoid(total)
    active = total * gate
    lane = lax.broadcasted_iota(jnp.int32, (size, SMALL), 1)
    small_grad = jnp.zeros((size, SMALL), f32)
    d_query_parts, d_key_parts, d_value_parts = [], [], []
    for head in range(heads):
        span = slice(head * width_v, (head + 1) * width_v)
        query_raw = active[:, head * width_k : (head + 1) * width_k]
        query_scale = lax.rsqrt(jnp.sum(query_raw * query_raw, axis=1, keepdims=True) + eps_norm)
        query_unit = query_raw * query_scale
        query = query_unit * width_k**-0.5
        key_at = heads * width_k + head * width_k
        key_raw = active[:, key_at : key_at + width_k]
        key_scale = lax.rsqrt(jnp.sum(key_raw * key_raw, axis=1, keepdims=True) + eps_norm)
        key = key_raw * key_scale
        value_at = 2 * heads * width_k + head * width_v
        value = active[:, value_at : value_at + width_v]
        pre_a, beta, rate, logdecay = gates(small, head, heads, decay_log, decay_bias)
        within, decay, carried, weight = decays(logdecay, meta, seg_row, row, col)
        wide = jnp.concatenate([carried] * (width_v // size), axis=1)
        keyed = decay * mm_nt(key, key, THREE)
        keyed = jnp.where(row > col, keyed, 0.0)
        scores = mm_nt(query, key, THREE) * decay
        entry = state_ref[0, head]
        inverse = inverse_ref[0, head]
        update = update_ref[:, span]
        output = raw_ref[:, span]
        scale = lax.rsqrt(jnp.mean(output * output, axis=1, keepdims=True) + eps_output)
        normed = output * scale
        pre = proj[:, mixed + head * width_v : mixed + (head + 1) * width_v]
        pre_gate = sigmoid(pre)
        silu = pre * pre_gate
        gain = gain_ref[0:1, span]
        d_gated = d_gated_ref[:, span]
        gained = d_gated * normed
        d_gain_ref[0:1, span] += jnp.sum(gained * silu, axis=0, keepdims=True)
        d_pre = gained * gain * (pre_gate * (1.0 + pre * (1.0 - pre_gate)))
        d_proj_ref[:, mixed + head * width_v : mixed + (head + 1) * width_v] = d_pre.astype(bf16)
        d_normed = d_gated * gain * silu
        d_output = scale * (
            d_normed - normed * jnp.mean(d_normed * normed, axis=1, keepdims=True)
        )
        d_exit = d_state[head]
        weighted = weight * key
        d_update = mm_tn(scores, d_output, THREE) + mm(weighted, d_exit, THREE)
        d_target = mm_tn(inverse, d_update, THREE)
        d_lower = jnp.where(row > col, -mm_nt(d_target, update, THREE), 0.0)
        d_scores = mm_nt(d_output, update, THREE)
        from_output = mm_nt(d_output, entry, THREE)
        from_target = mm_nt(d_target, entry, THREE)
        from_exit = mm_nt(update, d_exit, THREE)
        d_inner = d_scores * decay
        pair = d_lower * beta * decay
        d_query = carried * from_output + mm(d_inner, key, THREE)
        d_key = (
            mm_tn(d_inner, query, THREE)
            + weight * from_exit
            + mm(pair + pair.T, key, THREE)
            - beta * carried * from_target
        )
        d_value = beta * d_target
        d_state[head] = (
            wide[size - 1 : size] * d_exit
            + mm_tn(query, wide * d_output, THREE)
            - mm_tn(key, wide * d_value, THREE)
        )
        known_part = jnp.sum(key * from_target, axis=1, keepdims=True)
        carried_col = carried[:, 0:1]
        d_beta = (
            jnp.sum(d_target * value, axis=1, keepdims=True)
            - carried_col * known_part
            + jnp.sum(d_lower * keyed, axis=1, keepdims=True)
        )
        d_carried = jnp.sum(query * from_output, axis=1, keepdims=True) - beta * known_part
        d_spread = d_scores * scores + d_lower * (beta * keyed)
        d_weight = jnp.sum(weighted * from_exit, axis=1, keepdims=True)
        last = (row[:, 0:1] == size - 1).astype(f32)
        at_last = jnp.sum(d_weight, axis=0, keepdims=True) + carried_col[
            size - 1 : size
        ] * jnp.sum(jnp.sum(d_exit * entry, axis=1, keepdims=True), axis=0, keepdims=True)
        d_cumul = (
            jnp.sum(d_spread - d_spread.T, axis=1, keepdims=True)
            + d_carried * carried_col
            - d_weight
            + last * at_last
        )
        ones_above = (row <= col).astype(f32)
        d_logdecay = mm(ones_above, jnp.broadcast_to(d_cumul, (size, size)), EXACT)[:, 0:1]
        d_alpha = d_logdecay * rate * sigmoid(pre_a)
        d_scalars_ref[0:1, head : head + 1] += jnp.sum(
            d_logdecay * logdecay, axis=0, keepdims=True
        )
        d_scalars_ref[1:2, head : head + 1] += jnp.sum(d_alpha, axis=0, keepdims=True)
        small_grad = jnp.where(lane == head, d_alpha, small_grad)
        small_grad = jnp.where(lane == heads + head, d_beta * beta * (1.0 - beta), small_grad)
        d_query = d_query * width_k**-0.5
        d_query_parts.append(
            query_scale
            * (d_query - query_unit * jnp.sum(d_query * query_unit, axis=1, keepdims=True))
        )
        d_key_parts.append(key_scale * (d_key - key * jnp.sum(d_key * key, axis=1, keepdims=True)))
        d_value_parts.append(d_value)
    d_proj_ref[:, small_at : small_at + SMALL] = small_grad.astype(bf16)
    d_active = jnp.concatenate(d_query_parts + d_key_parts + d_value_parts, axis=1)
    d_total = d_active * (gate * (1.0 + total * (1.0 - gate)))
    d_block = taps[0:1] * d_total
    d_taps_ref[0:1, :] += jnp.sum(d_total * block, axis=0, keepdims=True)
    for offset in range(1, TAPS):
        d_taps_ref[offset : offset + 1, :] += jnp.sum(
            d_total * shifted[offset - 1], axis=0, keepdims=True
        )
        masked = d_total * meta[:, offset : offset + 1]
        joined = jnp.concatenate([masked, ahead[offset]], axis=0)
        d_block = d_block + taps[offset : offset + 1] * joined[offset : offset + size]
        ahead[offset] = masked[:HALO]
    d_proj_ref[:, :mixed] = d_block.astype(bf16)


def mixer_forward(proj, meta, seg_rows, taps, scalars, gain, heads, width_k, width_v):
    length = proj.shape[0]
    chunks = length // CHUNK
    mixed = heads * (2 * width_k + width_v)
    whole = lambda shape: pl.BlockSpec(shape, lambda c: (0,) * len(shape))
    rows = lambda width: pl.BlockSpec((CHUNK, width), lambda c: (c, 0))
    block4 = lambda a, b: pl.BlockSpec((1, heads, a, b), lambda c: (c, 0, 0, 0))
    return pl.pallas_call(
        partial(mixer_forward_kernel, heads, width_k, width_v),
        grid=(chunks,),
        in_specs=[
            rows(proj.shape[1]),
            rows(SMALL),
            pl.BlockSpec((8, CHUNK), lambda c: (c, 0)),
            whole(taps.shape),
            whole(scalars.shape),
            whole(gain.shape),
        ],
        out_specs=[
            rows(heads * width_v),
            rows(heads * width_v),
            rows(heads * width_v),
            block4(CHUNK, CHUNK),
            block4(width_k, width_v),
        ],
        out_shape=[
            jax.ShapeDtypeStruct((length, heads * width_v), bf16),
            jax.ShapeDtypeStruct((length, heads * width_v), f32),
            jax.ShapeDtypeStruct((length, heads * width_v), f32),
            jax.ShapeDtypeStruct((chunks, heads, CHUNK, CHUNK), f32),
            jax.ShapeDtypeStruct((chunks, heads, width_k, width_v), f32),
        ],
        scratch_shapes=[
            pltpu.VMEM((heads, width_k, width_v), f32),
            pltpu.VMEM((HALO, mixed), f32),
        ],
        name="mixer_forward",
    )(proj, meta, seg_rows, taps, scalars, gain)


def mixer_backward(
    proj, meta, seg_rows, taps, scalars, gain, d_gated, saved, heads, width_k, width_v
):
    length = proj.shape[0]
    chunks = length // CHUNK
    mixed = heads * (2 * width_k + width_v)
    last = chunks - 1
    per = CHUNK // HALO
    whole = lambda shape: pl.BlockSpec(shape, lambda c: (0,) * len(shape))
    rows = lambda width: pl.BlockSpec((CHUNK, width), lambda c: (last - c, 0))
    block4 = lambda a, b: pl.BlockSpec((1, heads, a, b), lambda c: (last - c, 0, 0, 0))
    raw, update, inverse, state = saved
    return pl.pallas_call(
        partial(mixer_backward_kernel, heads, width_k, width_v),
        grid=(chunks,),
        in_specs=[
            rows(proj.shape[1]),
            pl.BlockSpec(
                (HALO, proj.shape[1]), lambda c: (jnp.maximum((last - c) * per - 1, 0), 0)
            ),
            rows(SMALL),
            pl.BlockSpec((8, CHUNK), lambda c: (last - c, 0)),
            whole(taps.shape),
            whole(scalars.shape),
            whole(gain.shape),
            rows(heads * width_v),
            rows(heads * width_v),
            rows(heads * width_v),
            block4(CHUNK, CHUNK),
            block4(width_k, width_v),
        ],
        out_specs=[
            rows(proj.shape[1]),
            whole((8, mixed)),
            whole((8, heads * width_v)),
            whole((8, SMALL)),
        ],
        out_shape=[
            jax.ShapeDtypeStruct(proj.shape, bf16),
            jax.ShapeDtypeStruct((8, mixed), f32),
            jax.ShapeDtypeStruct((8, heads * width_v), f32),
            jax.ShapeDtypeStruct((8, SMALL), f32),
        ],
        scratch_shapes=[
            pltpu.VMEM((heads, width_k, width_v), f32),
            pltpu.VMEM((TAPS, HALO, mixed), f32),
        ],
        name="mixer_backward",
    )(proj, proj, meta, seg_rows, taps, scalars, gain, d_gated, raw, update, inverse, state)


def segment_tables(segment):
    length = segment.shape[0]
    columns = [segment.astype(f32)]
    for offset in range(1, TAPS):
        earlier = jnp.concatenate([jnp.full((offset,), -1, jnp.int32), segment[: length - offset]])
        columns.append((segment == earlier).astype(f32))
    ends = segment.reshape(-1, CHUNK)[:, -1]
    ends = jnp.concatenate([jnp.full((1,), -1, jnp.int32), ends[:-1]])
    columns.append((segment == jnp.repeat(ends, CHUNK)).astype(f32))
    meta = jnp.stack(columns, axis=1)
    meta = jnp.pad(meta, ((0, 0), (0, SMALL - meta.shape[1])))
    seg_rows = jnp.repeat(segment.astype(f32).reshape(-1, 1, CHUNK), 8, axis=1).reshape(-1, CHUNK)
    return meta, seg_rows


def row_scale(values):
    return lax.rsqrt(jnp.mean(values * values, axis=-1, keepdims=True) + eps_norm)


def norm_back(grad, normed, scale):
    return scale * (grad - normed * jnp.mean(grad * normed, axis=-1, keepdims=True))


def swap_core(value, axis, size):
    return lax.ppermute(value, axis, [(i, i ^ 1) for i in range(size)])


def swap_chip(value, axis, size):
    return lax.ppermute(value, axis, [(i, i ^ 2) for i in range(size)])


def pick(stacked, index, dim):
    return lax.dynamic_index_in_dim(stacked, index, dim, keepdims=False)


def interleave(mine, other, index, dim):
    first = index == 0
    return jnp.stack([jnp.where(first, mine, other), jnp.where(first, other, mine)], axis=dim)


def gather_rows(block, axis, size, chip, core):
    over = swap_chip(block, axis, size)
    pair = interleave(block, over, chip, 0)
    other = swap_core(pair, axis, size)
    return interleave(pair, other, core, 1).reshape(size * block.shape[0], block.shape[1])


def core_sum(partial_rows, axis, size, core):
    rows = partial_rows.shape[0] // size
    parts = partial_rows.reshape(2, 2, rows, partial_rows.shape[1])
    return pick(parts, core, 1) + swap_core(pick(parts, 1 - core, 1), axis, size)


def reduce_half(partial_rows, axis, size, core):
    mine = core_sum(partial_rows, axis, size, core).astype(bf16)
    return mine.astype(f32) + swap_chip(mine, axis, size).astype(f32)


def reduce_own(partial_rows, axis, size, chip, core):
    mine = core_sum(partial_rows, axis, size, core)
    away = swap_chip(pick(mine, 1 - chip, 0).astype(bf16), axis, size)
    return pick(mine, chip, 0) + away.astype(f32)


def join_halves(half, axis, size, core):
    other = swap_core(half, axis, size)
    return interleave(half, other, core, 1).reshape(-1, half.shape[-1])


def ring_place(index, size):
    return jnp.where(index % 2 == 0, index // 2, size - 1 - index // 2)


def ring_index(position, size):
    position = position % size
    return jnp.where(position < size // 2, 2 * position, 2 * (size - 1 - position) + 1)


def ring_moves(size):
    order = list(range(0, size, 2)) + list(range(size - 1, 0, -2))
    ahead = [(order[p], order[(p + 1) % size]) for p in range(size)]
    back = [(order[p], order[(p - 1) % size]) for p in range(size)]
    return ahead, back


def ring_gather(block, axis, size, place):
    if size > RING_MOST:
        return lax.all_gather(block, axis, axis=0, tiled=True)
    rows, width = block.shape
    ahead, back = ring_moves(size)
    split = rows // 2
    joined = jnp.zeros((size * rows, width), block.dtype)

    def put(joined, piece, position, offset=0):
        at = ring_index(position, size) * rows + offset
        return lax.dynamic_update_slice_in_dim(joined, piece, at, 0)

    joined = put(joined, block, place)
    from_back, from_ahead = block, block
    for step in range(1, size // 2):
        from_back = lax.ppermute(from_back, axis, ahead)
        from_ahead = lax.ppermute(from_ahead, axis, back)
        joined = put(joined, from_back, place - step + size)
        joined = put(joined, from_ahead, place + step)
    top = lax.ppermute(from_back[:split], axis, ahead)
    bottom = lax.ppermute(from_ahead[split:], axis, back)
    joined = put(joined, top, place + size // 2)
    return put(joined, bottom, place + size // 2, split)


def ring_scatter(part_of, axis, size, place):
    if size > RING_MOST:
        whole = jnp.concatenate([part_of(index).astype(bf16) for index in range(size)], axis=0)
        return lax.psum_scatter(whole, axis, scatter_dimension=0, tiled=True).astype(f32)
    ahead, back = ring_moves(size)
    far = part_of(ring_index(place + size // 2, size))
    split = far.shape[0] // 2
    going = lax.ppermute(far[:split].astype(bf16), axis, ahead)
    coming = lax.ppermute(far[split:].astype(bf16), axis, back)
    for step in range(size // 2 - 1, 0, -1):
        forth = part_of(ring_index(place + step, size))
        fro = part_of(ring_index(place - step + size, size))
        if going.shape[0] == split:
            forth = jnp.concatenate([forth[:split] + going.astype(f32), forth[split:]], axis=0)
            fro = jnp.concatenate([fro[:split], fro[split:] + coming.astype(f32)], axis=0)
        else:
            forth = forth + going.astype(f32)
            fro = fro + coming.astype(f32)
        going = lax.ppermute(forth.astype(bf16), axis, ahead)
        coming = lax.ppermute(fro.astype(bf16), axis, back)
    return part_of(ring_index(place, size)) + going.astype(f32) + coming.astype(f32)


def butterfly_sum(value, axis, size):
    step = 1
    while step < size:
        value = value + lax.ppermute(value, axis, [(i, i ^ step) for i in range(size)])
        step = 2 * step
    return value


def per_device(
    tokens,
    segment_ids,
    norm_gain_mixer,
    query_weight,
    key_weight,
    value_weight,
    gate_weight,
    alpha_weight,
    beta_weight,
    conv_query,
    conv_key,
    conv_value,
    decay_log,
    decay_bias,
    output_gain,
    output_weight,
    norm_gain_ffn,
    ffn_gate,
    ffn_up,
    ffn_down,
    grad_block,
):
    n_dp = lax.axis_size("dp")
    n_t = lax.axis_size("tensor")
    place = lax.axis_index("tensor")
    chip, core = place // 2, place % 2
    rows, width = tokens.shape
    owned = query_weight.shape[0]
    heads = decay_log.shape[0]
    width_k = query_weight.shape[1] // heads
    width_v = value_weight.shape[1] // heads
    hidden_units = ffn_gate.shape[1]
    mixed = heads * (2 * width_k + width_v)
    inner = heads * width_v
    gather_weights = lambda block: lax.all_gather(block, "dp", axis=0, tiled=True)

    thin = [
        alpha_weight,
        beta_weight,
        norm_gain_mixer.reshape(owned, 1),
        norm_gain_ffn.reshape(owned, 1),
        conv_query.reshape(owned, -1),
        conv_key.reshape(owned, -1),
        conv_value.reshape(owned, -1),
        jnp.pad(output_gain.reshape(-1), (0, owned - output_gain.size)).reshape(owned, 1),
    ]
    thin = jnp.concatenate(thin, axis=1)
    thin = jnp.pad(thin, ((0, 0), (0, SMALL - thin.shape[1])))
    dp_place = lax.axis_index("dp")
    ring_at = ring_place(dp_place, n_dp)
    weights = ring_gather(
        jnp.concatenate([query_weight, key_weight, value_weight, gate_weight, thin], axis=1),
        "dp",
        n_dp,
        ring_at,
    )
    later = gather_weights(
        jnp.concatenate([ffn_gate, ffn_up, ffn_down.T, output_weight.T], axis=1)
    )
    gate_up = later[:, : 2 * hidden_units]
    down_t = later[:, 2 * hidden_units : 3 * hidden_units]
    out_t = later[:, 3 * hidden_units :]

    tokens_full = gather_rows(tokens, "tensor", n_t, chip, core)
    grad_full = gather_rows(grad_block, "tensor", n_t, chip, core)

    thin_t = weights[:, mixed + inner :].astype(f32).T
    gain_mix = thin_t[2 * heads : 2 * heads + 1]
    gain_ffn = thin_t[2 * heads + 1 : 2 * heads + 2]

    def taps_of(first, count, size):
        flat = thin_t[first : first + count].T
        return flat.reshape(n_dp, TAPS, heads, size // n_dp).transpose(1, 2, 0, 3).reshape(TAPS, -1)

    at = 2 * heads + 2
    taps = jnp.concatenate(
        [taps_of(at, 1, width_k), taps_of(at + 1, 1, width_k), taps_of(at + 2, 2, width_v)], axis=1
    )
    taps = jnp.pad(taps, ((0, 8 - TAPS), (0, 0)))
    out_gain = thin_t[at + 4].reshape(n_dp, owned)[:, : output_gain.size]
    out_gain = out_gain.reshape(n_dp, heads, width_v // n_dp).transpose(1, 0, 2).reshape(1, inner)
    out_gain = jnp.pad(out_gain, ((0, 7), (0, 0)))
    scalars = jnp.pad(jnp.stack([decay_log, decay_bias]), ((0, 6), (0, SMALL - heads)))
    meta, seg_rows = segment_tables(segment_ids)

    resid_in = tokens_full.astype(f32)
    mixer_norm = resid_in * row_scale(resid_in)
    mixer_in = (mixer_norm * gain_mix).astype(bf16)
    proj = mm(mixer_in, weights)
    sizes = (heads, width_k, width_v)
    out_gated, *saved = mixer_forward(proj, meta, seg_rows, taps, scalars, out_gain, *sizes)
    mixer_out = reduce_half(mm_nt(out_gated, out_t), "tensor", n_t, core)

    def half_of(full):
        return pick(full.reshape(2, 2, rows, width), core, 1)

    resid = half_of(tokens_full).astype(f32) + mixer_out
    ffn_rms = row_scale(resid)
    ffn_norm = resid * ffn_rms
    ffn_in = join_halves((ffn_norm * gain_ffn).astype(bf16), "tensor", n_t, core)

    pre = mm(ffn_in, gate_up)
    gate_pre, up_pre = pre[:, :hidden_units], pre[:, hidden_units:]
    sigma = jax.nn.sigmoid(gate_pre)
    silu = gate_pre * sigma
    hidden = (silu * up_pre).astype(bf16)
    d_hidden = mm(grad_full, down_t)
    d_gate = d_hidden * up_pre * sigma * (1.0 + gate_pre * (1.0 - sigma))
    d_pre = jnp.concatenate([d_gate.astype(bf16), (d_hidden * silu).astype(bf16)], axis=1)
    d_ffn_in = reduce_half(mm_nt(d_pre, gate_up), "tensor", n_t, core)
    d_resid = half_of(grad_full).astype(f32) + norm_back(d_ffn_in * gain_ffn, ffn_norm, ffn_rms)
    d_mix = join_halves(d_resid.astype(bf16), "tensor", n_t, core)
    ffn_out = reduce_own(mm_nt(hidden, down_t), "tensor", n_t, chip, core)
    block_output = (pick(resid, chip, 0) + ffn_out).astype(bf16)
    ffn_gain_part = jnp.sum(pick(d_ffn_in * ffn_norm, chip, 0), axis=0)

    def scatter(blocks):
        joined = jnp.concatenate([block.astype(bf16) for block in blocks], axis=1)
        return lax.psum_scatter(joined, "dp", scatter_dimension=0, tiled=True).astype(f32)

    ffn_grads = scatter([mm_tn(ffn_in, d_pre), mm_tn(grad_full, hidden)])

    d_gated = mm(d_mix, out_t)
    d_proj, d_taps, d_gain, d_scalars = mixer_backward(
        proj, meta, seg_rows, taps, scalars, out_gain, d_gated, saved, *sizes
    )

    def mixer_part(index):
        left = lax.dynamic_slice_in_dim(d_mix, index * owned, owned, 1)
        right = lax.dynamic_slice_in_dim(mixer_in, index * owned, owned, 1)
        return jnp.concatenate([mm_tn(left, out_gated), mm_tn(right, d_proj)], axis=1)

    mixer_grads = ring_scatter(mixer_part, "dp", n_dp, ring_at)
    d_mixer_in = reduce_own(mm_nt(d_proj, weights), "tensor", n_t, chip, core)
    own_tokens = tokens.astype(f32)
    own_rms = row_scale(own_tokens)
    own_norm = own_tokens * own_rms
    mix_gain_part = jnp.sum(d_mixer_in * own_norm, axis=0)
    tokens_grad = pick(d_resid, chip, 0) + norm_back(d_mixer_in * gain_mix, own_norm, own_rms)

    gains = butterfly_sum(jnp.stack([mix_gain_part, ffn_gain_part]), "tensor", n_t)
    rest = jnp.concatenate([d_gain[0], d_scalars[0, :heads], d_scalars[1, :heads]])
    rest = jnp.pad(rest, (0, mixed - rest.size)).reshape(1, mixed)
    pad = jnp.pad(gains, ((0, 0), (0, mixed - width)))
    sums = butterfly_sum(jnp.concatenate([d_taps[:TAPS], pad, rest], axis=0), "dp", n_dp)
    taps_grad, rest = sums[:TAPS], sums[TAPS + 2]
    own_gains = lax.dynamic_slice_in_dim(sums[TAPS : TAPS + 2], dp_place * owned, owned, 1)
    mix_gain_grad, ffn_gain_grad = own_gains[0], own_gains[1]

    def own_columns(part, size):
        split = part.reshape(-1, heads, n_dp, size // n_dp)
        return lax.dynamic_index_in_dim(split, dp_place, 2, keepdims=False)

    key_at, value_at = heads * width_k, 2 * heads * width_k
    conv_grads = (
        own_columns(taps_grad[:, :key_at], width_k),
        own_columns(taps_grad[:, key_at:value_at], width_k),
        own_columns(taps_grad[:, value_at:], width_v),
    )
    projected = mixer_grads[:, inner:]
    return (
        block_output,
        tokens_grad,
        mix_gain_grad,
        projected[:, :key_at],
        projected[:, key_at:value_at],
        projected[:, value_at:mixed],
        projected[:, mixed : mixed + inner],
        projected[:, mixed + inner : mixed + inner + heads],
        projected[:, mixed + inner + heads : mixed + inner + 2 * heads],
        *conv_grads,
        rest[inner : inner + heads],
        rest[inner + heads : inner + 2 * heads],
        own_columns(rest[:inner].reshape(1, -1), width_v)[0],
        mixer_grads[:, :inner].T,
        ffn_gain_grad,
        ffn_grads[:, :hidden_units],
        ffn_grads[:, hidden_units : 2 * hidden_units],
        ffn_grads[:, 2 * hidden_units :].T,
    )


def solution(mesh):
    by_rows = P(("dp", "tensor"), None)
    tiled, turned = P("dp", "tensor"), P("tensor", "dp")
    conv = P(None, "tensor", "dp")
    weights_in = (tiled,) * 6
    return jax.shard_map(
        per_device,
        mesh=mesh,
        in_specs=(
            by_rows,
            P("dp"),
            P("dp"),
            *weights_in,
            conv,
            conv,
            conv,
            P("tensor"),
            P("tensor"),
            turned,
            turned,
            P("dp"),
            tiled,
            tiled,
            turned,
            by_rows,
        ),
        out_specs=(
            by_rows,
            by_rows,
            P("dp"),
            *weights_in,
            conv,
            conv,
            conv,
            P("tensor"),
            P("tensor"),
            turned,
            turned,
            P("dp"),
            tiled,
            tiled,
            turned,
        ),
        check_vma=False,
    )
```
